1024 devices in a mesh: gx: 64 (over z, y_lo), gz: 4 (over x), ta: 4 (over y_hi, core).
Axes of the slice: x: 4, y: 4 (y_hi: 2, y_lo: 2; y = y_hi * 2 + y_lo), z: 32, core: 2. Of those that a mesh axis runs over, the one named last changes fastest.
Arguments:
- rhs: float32 [64, 2, 2, 16, 16, 8, 64], P('gx', None, None, 'gz', 'ta'), may hold values from -20 to 20
- self_coupling: bfloat16 [64, 2, 2, 16, 16, 64, 64], P('gx', None, None, 'gz', 'ta'), may hold values from -0.75 to 0.75
- hopping: bfloat16 [4, 64, 2, 2, 16, 16, 64, 64], P(None, 'gx', None, None, 'gz', 'ta'), may hold values from -0.5 to 0.5
Outputs:
- solution: float32 [64, 2, 2, 16, 16, 8, 64], P('gx', None, None, 'gz', 'ta')
- residual: float32 [64, 2, 2, 16, 16, 8, 64], P('gx', None, None, 'gz', 'ta')
The draws below stay inside these ranges and needn't reach their ends.
All inputs are finite; a program needn't handle non-finite values.
Results may differ from the reference program's by a relative error of at most 0.0087.
Values may be sent and summed in bfloat16 or wider, within the bound.
A program may use at most 32 MiB of HBM per device.

```python
import jax
import jax.numpy as jnp
from jax import lax

C = 64
R = 8
BX = 2
BY = 2
BZ = 4
BT = 4
MR_STEPS = 2
NB = 64
PY = 8
LZ = 16
LT = 16


def draw_rhs(key, part):
    key_noise, key_spread = jax.random.split(key, 2)
    full_shape = (NB, BX, BY, LZ, LT, R, C)
    sample = jnp.clip(jax.random.normal(key_noise, full_shape, jnp.float32), -4.0, 4.0)
    spread = jax.random.uniform(key_spread, (NB, BX, BY, LZ, LT, 1, 1), jnp.float32, 0.0, 1.0)
    rising = jnp.arange(NB, dtype=jnp.float32).reshape(NB, 1, 1, 1, 1, 1, 1) / (NB - 1)
    factor = 10.0 ** spread * 3.0 ** rising / 6.0
    return sample * factor


def shard_levels(own_key, shape, cuts, low, top_value):
    def one(axis_at, blocks):
        heights = jax.random.uniform(jax.random.fold_in(jax.random.fold_in(own_key, 6), axis_at), (blocks,), jnp.float32, low / len(cuts), top_value / len(cuts))
        return jnp.repeat(jnp.exp(heights), shape[axis_at] // blocks).reshape((-1,) + (1,) * (len(shape) - axis_at - 1))

    gain = one(*cuts[0])
    for cut in cuts[1:]:
        gain = gain * one(*cut)
    return gain


def centred(rng, dims, deviation, reach, pieces=(), held_as=jnp.bfloat16):
    values = deviation * jax.random.normal(rng, dims, jnp.float32)
    if pieces:
        values = values * shard_levels(rng, dims, pieces, -0.22, 0.18)
    return jnp.clip(values, -reach, reach).astype(held_as)


def setup_inputs(seed: int = 0) -> dict:
    splits = jax.random.split(jax.random.key(seed), 4)
    return {
        "rhs": draw_rhs(jax.random.fold_in(splits[3], 71), 0),
        "self_coupling": centred(splits[1], (NB, BX, BY, LZ, LT, C, C), C ** -0.5, 0.75, ((0, 64), (3, 4), (4, 4))),
        "hopping": centred(splits[2], (4, NB, BX, BY, LZ, LT, C, C), (2 * C) ** -0.5, 0.5, ((1, 64), (4, 4), (5, 4))),
    }


forward_form = "xyztab,xyztrb->xyztra"
backward_form = "xyztab,xyztra->xyztrb"


def site_product(links, field_bf, form):
    def single(operands):
        return jnp.einsum(form, operands[0].astype(jnp.float32), operands[1].astype(jnp.float32))
    return lax.map(single, (links, field_bf))


def block_step(direction):
    return PY if direction == 0 else 1


def ahead_of(values, direction):
    if direction >= 2:
        return jnp.roll(values, -1, axis=direction + 1)
    axis = direction + 1
    extent = values.shape[axis]
    moved = jnp.roll(values, -block_step(direction), axis=0)
    inner = lax.slice_in_dim(values, 1, extent, axis=axis)
    edge = lax.slice_in_dim(moved, 0, 1, axis=axis)
    return jnp.concatenate([inner, edge], axis=axis)


def behind_of(values, direction):
    if direction >= 2:
        return jnp.roll(values, 1, axis=direction + 1)
    axis = direction + 1
    extent = values.shape[axis]
    moved = jnp.roll(values, block_step(direction), axis=0)
    inner = lax.slice_in_dim(values, 0, extent - 1, axis=axis)
    edge = lax.slice_in_dim(moved, extent - 1, extent, axis=axis)
    return jnp.concatenate([edge, inner], axis=axis)


def rim_masks():
    coords = [jnp.arange(BX).reshape(1, BX, 1, 1, 1, 1, 1),
              jnp.arange(BY).reshape(1, 1, BY, 1, 1, 1, 1),
              (jnp.arange(LZ) % BZ).reshape(1, 1, 1, LZ, 1, 1, 1),
              (jnp.arange(LT) % BT).reshape(1, 1, 1, 1, LT, 1, 1)]
    widths = [BX, BY, BZ, BT]
    upward = [(coords[direction] != widths[direction] - 1).astype(jnp.float32) for direction in range(4)]
    downward = [(coords[direction] != 0).astype(jnp.float32) for direction in range(4)]
    return upward, downward


def apply_operator(vector, self_coupling, hopping, confined):
    field_bf = vector.astype(jnp.bfloat16)
    chirality = jnp.where(jnp.arange(C) < C // 2, 1.0, -1.0).astype(jnp.bfloat16)
    result = 4.0 * vector + site_product(self_coupling, field_bf, forward_form)
    upward, downward = rim_masks()
    for direction in range(4):
        ahead_field = ahead_of(field_bf, direction)
        forward_term = site_product(hopping[direction], ahead_field, forward_form)
        back_term = (chirality * site_product(hopping[direction], chirality * field_bf, backward_form)).astype(jnp.bfloat16)
        behind = behind_of(back_term, direction).astype(jnp.float32)
        if confined:
            forward_term = forward_term * upward[direction]
            behind = behind * downward[direction]
        result = result + forward_term + behind
    return result


def mesh_dot(left, right):
    return jnp.sum(left * right, axis=(0, 1, 2, 3, 4, 6))[:, None]


def domain_ratio(mapped, remain):
    split_shape = (NB, BX, BY, LZ // BZ, BZ, LT // BT, BT, R, C)
    numer_sum = jnp.sum((mapped * remain).reshape(split_shape), axis=(1, 2, 4, 6, 8), keepdims=True)
    bottom = jnp.sum((mapped * mapped).reshape(split_shape), axis=(1, 2, 4, 6, 8), keepdims=True)
    return jnp.broadcast_to(numer_sum / bottom, split_shape).reshape(mapped.shape)


def smoothing(source, self_coupling, hopping):
    remain = source
    update = jnp.zeros_like(source)
    for repeat_index in range(MR_STEPS):
        mapped = apply_operator(remain, self_coupling, hopping, True)
        weight = domain_ratio(mapped, remain)
        update = update + weight * remain
        remain = remain - weight * mapped
    return update


def reference(rhs, self_coupling, hopping):
    direction_zero = smoothing(rhs, self_coupling, hopping)
    mapped_zero = apply_operator(direction_zero, self_coupling, hopping, False)
    norm_zero = mesh_dot(mapped_zero, mapped_zero)
    alpha_first = mesh_dot(mapped_zero, rhs) / norm_zero
    solution_one = alpha_first * direction_zero
    residual_one = rhs - alpha_first * mapped_zero
    direction_raw = smoothing(residual_one, self_coupling, hopping)
    mapped_raw = apply_operator(direction_raw, self_coupling, hopping, False)
    beta_value = mesh_dot(mapped_zero, mapped_raw) / norm_zero
    direction_one = direction_raw - beta_value * direction_zero
    mapped_one = mapped_raw - beta_value * mapped_zero
    alpha_second = mesh_dot(mapped_one, residual_one) / mesh_dot(mapped_one, mapped_one)
    solution = solution_one + alpha_second * direction_one
    residual = residual_one - alpha_second * mapped_one
    return solution, residual
```

```python
import functools

import jax
import jax.numpy as jnp
from jax import lax
from jax.experimental import pallas as pl
from jax.experimental.pallas import tpu as pltpu
from jax.sharding import PartitionSpec as P

MESH = pl.DeviceIdType.MESH
EXT = (2, 2, 4, 4)
F32 = jnp.float32
BF16 = jnp.bfloat16
STAGES = (7, 3, 3, 8)
SLOTS = sum(STAGES)


def part(direction, low, high):
    return tuple(slice(low, high) if d == direction else slice(None) for d in range(4))


def flat(values):
    return values.reshape((-1,) + values.shape[4:])


def forward_dot(fields, links):
    return lax.dot_general(fields, links, (((2,), (2,)), ((0,), (0,))), preferred_element_type=F32)


def backward_dot(fields, links):
    return lax.dot_general(fields, links, (((2,), (1,)), ((0,), (0,))), preferred_element_type=F32)


def whole(mesh_size, value):
    return lax.rem(value + mesh_size, mesh_size)


class Place:
    def __init__(self, sizes, row_len):
        self.sizes = sizes
        self.row_len = row_len
        self.gx = lax.axis_index("gx")
        self.gz = lax.axis_index("gz")
        self.ta = lax.axis_index("ta")

    def at(self, gx=0, gz=0, ta=0, flip_gx=0, flip_ta=0):
        x = whole(self.sizes["gx"], self.gx + gx)
        z = whole(self.sizes["gz"], self.gz + gz)
        t = whole(self.sizes["ta"], self.ta + ta)
        if flip_gx:
            x = x + 1 - 2 * lax.rem(x, 2)
        if flip_ta & 1:
            t = t + 1 - 2 * lax.rem(t, 2)
        if flip_ta & 2:
            t = whole(self.sizes["ta"], t + 2)
        return {"gx": x, "gz": z, "ta": t}

    def ahead(self, direction, sign):
        if direction == 0:
            return self.at(gx=sign * self.row_len)
        if direction == 1:
            return self.at(gx=sign)
        if direction == 2:
            return self.at(gz=sign)
        return self.at(ta=sign)

    def stage(self, index):
        if index == 0:
            out = [self.at(gz=k, flip_ta=c) for k in range(4) for c in range(2)]
            return out[1:]
        if index == 1:
            return [self.at(flip_gx=1), self.at(flip_ta=2), self.at(flip_gx=1, flip_ta=2)]
        if index == 2:
            return [self.at(gx=2), self.at(gx=-2), self.at(gx=-4)]
        return [self.at(gx=2 * k) for k in (2, -2, 6, -6, 10, -10, 14, -14)]


def on_device(sizes, row_len, rhs_hbm, self_hbm, hop_hbm, sol_ref, res_ref,
              rhs, links, hops, vb, vc, acc_f, acc_b, m0, m1, r1, d0, z_field, rt, lt, lz,
              lt2, lz2, d1, send_xy, send_zt, got_xy, got_zt, rows_out, rows_in,
              load_sem, halo_send, halo_recv, sum_send, sum_recv):
    place = Place(sizes, row_len)
    loads = [pltpu.make_async_copy(rhs_hbm, rhs, load_sem.at[0]),
             pltpu.make_async_copy(self_hbm, links, load_sem.at[1])]
    for d in range(4):
        loads.append(pltpu.make_async_copy(hop_hbm.at[d], hops.at[d], load_sem.at[2 + d]))
    for load in loads:
        load.start()

    greeted = [place.ahead(d, sign) for d in range(4) for sign in (1, -1)]
    greeted += place.stage(0) + place.stage(1) + [place.at(gx=2), place.at(gx=-2)] + place.stage(3)
    barrier = pltpu.get_barrier_semaphore()
    for other in greeted:
        pl.semaphore_signal(barrier, inc=1, device_id=other, device_id_type=MESH)

    lane = lax.broadcasted_iota(jnp.int32, (1, 1, 64), 2)
    chi = jnp.where(lane < 32, 1.0, -1.0).astype(F32)
    lane_r = lax.broadcasted_iota(jnp.int32, (8, 128), 1)
    sub_r = lax.broadcasted_iota(jnp.int32, (8, 128), 0)

    def dot_sum(a, b):
        return jnp.sum(jnp.sum(flat(a) * flat(b), axis=0), axis=-1, keepdims=True)

    def to_row(columns):
        spread = jnp.zeros((8, 128), F32)
        for k, column in enumerate(columns):
            spread = jnp.where(lane_r == 8 * k + sub_r, column, spread)
        return jnp.sum(spread, axis=0, keepdims=True)

    def from_row(row, k):
        return jnp.sum(jnp.where(lane_r == 8 * k + sub_r, row, 0.0), axis=1, keepdims=True)

    def load_fields(fields):
        pieces = []
        for field in fields:
            top = field.astype(BF16).astype(F32)
            pieces += [top, field - top]
        stacked = jnp.concatenate(pieces, axis=4)
        height = 16 * len(fields)
        vb[..., 0:height, :] = stacked.astype(BF16)
        vc[..., 0:height, :] = (stacked * chi).astype(BF16)
        return height

    def local_apply(fields, outs, first=False):
        h = load_fields(fields)
        if first:
            loads[1].wait()
        acc_f[..., 0:h, :] = forward_dot(flat(vb[..., 0:h, :]), flat(links[...])).reshape(EXT + (h, 64))
        acc_b[..., 0:h, :] = jnp.zeros(EXT + (h, 64), F32)
        for d in range(4):
            if first:
                loads[2 + d].wait()
            low, high = part(d, 0, EXT[d] - 1), part(d, 1, EXT[d])
            block = flat(hops[(d,) + low])
            shape = tuple(EXT[k] - (k == d) for k in range(4)) + (h, 64)
            span = (slice(0, h), slice(None))
            acc_f[low + span] += forward_dot(flat(vb[high + span]), block).reshape(shape)
            acc_b[high + span] += backward_dot(flat(vc[low + span]), block).reshape(shape)
        for k, (field, out) in enumerate(zip(fields, outs)):
            a, b = slice(16 * k, 16 * k + 8), slice(16 * k + 8, 16 * k + 16)
            total_f = acc_f[..., a, :] + acc_f[..., b, :]
            total_b = acc_b[..., a, :] + acc_b[..., b, :]
            out[...] = 4.0 * field + total_f + chi * total_b

    def face_refs(store, around, d, kind):
        xy, zt = store
        return (xy if d < 2 else zt).at[around, d % 2, kind]

    def pack(face):
        half = face.shape[0] // 2
        return jnp.concatenate([face[:half], face[half:]], axis=-1).astype(BF16)

    def unpack(ref):
        both = ref[...].astype(F32)
        return jnp.concatenate([both[..., :64], both[..., 64:]], axis=0)

    def halo_copy(around, d, kind):
        slot = (around * 4 + d) * 2 + kind
        return pltpu.make_async_remote_copy(
            src_ref=face_refs((send_xy, send_zt), around, d, kind),
            dst_ref=face_refs((got_xy, got_zt), around, d, kind),
            send_sem=halo_send.at[slot],
            recv_sem=halo_recv.at[slot],
            device_id=place.ahead(d, -1 if kind == 0 else 1),
            device_id_type=MESH,
        )

    def halo_start(around, field):
        for d in range(4):
            low = flat(field[part(d, 0, 1)])
            face_refs((send_xy, send_zt), around, d, 0)[...] = pack(low)
            halo_copy(around, d, 0).start()
            top = part(d, EXT[d] - 1, EXT[d])
            flipped = (flat(field[top]) * chi).astype(BF16)
            back = chi * backward_dot(flipped, flat(hops[(d,) + top]))
            face_refs((send_xy, send_zt), around, d, 1)[...] = pack(back)
            halo_copy(around, d, 1).start()

    def halo_finish(around, out):
        for d in (2, 3, 1, 0):
            shape = tuple(1 if k == d else EXT[k] for k in range(4)) + (8, 64)
            halo_copy(around, d, 0).wait_recv()
            top = part(d, EXT[d] - 1, EXT[d])
            ahead = unpack(face_refs((got_xy, got_zt), around, d, 0)).astype(BF16)
            out[top] += forward_dot(ahead, flat(hops[(d,) + top])).reshape(shape)
            halo_copy(around, d, 1).wait_recv()
            low = part(d, 0, 1)
            out[low] += unpack(face_refs((got_xy, got_zt), around, d, 1)).reshape(shape)

    def sum_copies(around, index):
        base = around * SLOTS + sum(STAGES[:index])
        return [
            pltpu.make_async_remote_copy(
                src_ref=rows_out.at[around * 4 + index],
                dst_ref=rows_in.at[base + k],
                send_sem=sum_send.at[base + k],
                recv_sem=sum_recv.at[base + k],
                device_id=other,
                device_id_type=MESH,
            )
            for k, other in enumerate(place.stage(index))
        ]

    def sum_start(around, index, row):
        rows_out[around * 4 + index] = row
        copies = sum_copies(around, index)
        for copy in copies:
            copy.start()
        return copies

    def sum_finish(around, index, copies, row):
        base = around * SLOTS + sum(STAGES[:index])
        total = row
        for k, copy in enumerate(copies):
            copy.wait_recv()
            got = rows_in[base + k]
            total = got if total is None else total + got
        return total

    def mesh_sum(around, row, meanwhile=None):
        for index in range(4):
            copies = sum_start(around, index, row)
            kept = row if index < 3 else None
            if index == 3 and meanwhile is not None:
                meanwhile()
            row = sum_finish(around, index, copies, kept)
        return row

    loads[0].wait()
    source = rhs[...]
    local_apply([source], [m0], first=True)
    first = m0[...]
    source = rhs[...]
    weight_a = dot_sum(first, source) / dot_sum(first, first)
    r1[...] = source - weight_a * first
    local_apply([r1[...]], [m1])
    second, left = m1[...], r1[...]
    weight_b = dot_sum(second, left) / dot_sum(second, second)
    d0[...] = weight_a * rhs[...] + weight_b * left
    pl.semaphore_wait(barrier, len(greeted))
    halo_start(0, d0)
    z_field[...] = weight_a * m0[...] + weight_b * m1[...]
    halo_finish(0, z_field)

    zero = z_field[...]
    part_zr, part_zz = dot_sum(zero, rhs[...]), dot_sum(zero, zero)
    centre = jnp.where(part_zz > 0.0, part_zr / jnp.where(part_zz > 0.0, part_zz, 1.0), 0.0)

    def meanwhile():
        rt[...] = rhs[...] - centre * z_field[...]
        local_apply([rt[...], z_field[...]], [lt, lz])
        local_apply([lt[...], lz[...]], [lt2, lz2])

    sums = mesh_sum(0, to_row([part_zr, part_zz]), meanwhile)
    sum_zz = from_row(sums, 1)
    alpha = from_row(sums, 0) / sum_zz
    shift = alpha - centre
    r1[...] = rhs[...] - alpha * z_field[...]
    m0[...] = lt[...] - shift * lz[...]
    first = m0[...]
    weight_a = dot_sum(first, r1[...]) / dot_sum(first, first)
    m1[...] = m0[...] - weight_a * (lt2[...] - shift * lz2[...])
    rt[...] = r1[...] - weight_a * m0[...]
    second = m1[...]
    weight_b = dot_sum(second, rt[...]) / dot_sum(second, second)
    d1[...] = weight_a * r1[...] + weight_b * rt[...]
    halo_start(1, d1)
    lz[...] = weight_a * m0[...] + weight_b * m1[...]
    halo_finish(1, lz)

    raw = lz[...]
    columns = [dot_sum(z_field[...], raw), dot_sum(raw, r1[...]), dot_sum(raw, raw),
               dot_sum(z_field[...], r1[...])]
    sums = mesh_sum(1, to_row(columns))
    cross, onto, square, kept = [from_row(sums, k) for k in range(4)]
    beta = cross / sum_zz
    alpha_b = (onto - beta * kept) / (square - beta * (2.0 * cross - beta * sum_zz))
    sol_ref[...] = alpha * d0[...] + alpha_b * (d1[...] - beta * d0[...])
    res_ref[...] = r1[...] - alpha_b * (lz[...] - beta * z_field[...])

    for around in range(2):
        for d in range(4):
            for kind in range(2):
                halo_copy(around, d, kind).wait_send()
        for index in range(4):
            for copy in sum_copies(around, index):
                copy.wait_send()


def solution(mesh):
    sizes = dict(mesh.shape)
    row_len = min(8, max(2, sizes["gx"] // 8))

    def step(rhs, self_coupling, hopping):
        field = EXT + (8, 64)
        vmem = pl.BlockSpec(memory_space=pltpu.VMEM)
        hbm = pl.BlockSpec(memory_space=pl.ANY)
        fields = [pltpu.VMEM(field, F32)] * 10
        sol, res = pl.pallas_call(
            functools.partial(on_device, sizes, row_len),
            out_shape=[jax.ShapeDtypeStruct(field, F32)] * 2,
            in_specs=[hbm] * 3,
            out_specs=[vmem] * 2,
            scratch_shapes=[
                pltpu.VMEM(field, F32),
                pltpu.VMEM(EXT + (64, 64), BF16),
                pltpu.VMEM((4,) + EXT + (64, 64), BF16),
                pltpu.VMEM(EXT + (32, 64), BF16),
                pltpu.VMEM(EXT + (32, 64), BF16),
                pltpu.VMEM(EXT + (32, 64), F32),
                pltpu.VMEM(EXT + (32, 64), F32),
                *fields,
                pltpu.VMEM(field, F32),
                pltpu.VMEM((2, 2, 2, 16, 8, 128), BF16),
                pltpu.VMEM((2, 2, 2, 8, 8, 128), BF16),
                pltpu.VMEM((2, 2, 2, 16, 8, 128), BF16),
                pltpu.VMEM((2, 2, 2, 8, 8, 128), BF16),
                pltpu.VMEM((8, 1, 128), F32),
                pltpu.VMEM((2 * SLOTS, 1, 128), F32),
                pltpu.SemaphoreType.DMA((6,)),
                pltpu.SemaphoreType.DMA((16,)),
                pltpu.SemaphoreType.DMA((16,)),
                pltpu.SemaphoreType.DMA((2 * SLOTS,)),
                pltpu.SemaphoreType.DMA((2 * SLOTS,)),
            ],
            compiler_params=pltpu.CompilerParams(collective_id=0, has_side_effects=True),
        )(rhs[0], self_coupling[0], hopping[:, 0])
        return sol[None], res[None]

    whole_spec = P("gx", None, None, "gz", "ta", None, None)
    return jax.shard_map(
        step,
        mesh=mesh,
        in_specs=(whole_spec, whole_spec, P(None, "gx", None, None, "gz", "ta", None, None)),
        out_specs=(whole_spec, whole_spec),
        check_vma=False,
    )
```

```python
import functools

import jax
import jax.numpy as jnp
from jax import lax
from jax.experimental import pallas as pl
from jax.experimental.pallas import tpu as pltpu
from jax.sharding import PartitionSpec as P

MESH = pl.DeviceIdType.MESH
EXT = (2, 2, 4, 4)
F32 = jnp.float32
BF16 = jnp.bfloat16
STAGES = (1, 15, 31)
SLOTS = sum(STAGES)


def part(direction, low, high):
    return tuple(slice(low, high) if d == direction else slice(None) for d in range(4))


def flat(values):
    return values.reshape((-1,) + values.shape[4:])


def forward_dot(fields, links):
    return lax.dot_general(fields, links, (((2,), (2,)), ((0,), (0,))), preferred_element_type=F32)


def backward_dot(fields, links):
    return lax.dot_general(fields, links, (((2,), (1,)), ((0,), (0,))), preferred_element_type=F32)


def whole(mesh_size, value):
    return lax.rem(value + mesh_size, mesh_size)


class Place:
    def __init__(self, sizes, row_len):
        self.sizes = sizes
        self.row_len = row_len
        self.gx = lax.axis_index("gx")
        self.gz = lax.axis_index("gz")
        self.ta = lax.axis_index("ta")

    def at(self, gx=0, gz=0, ta=0, flip_gx=0, flip_ta=0):
        x = whole(self.sizes["gx"], self.gx + gx)
        z = whole(self.sizes["gz"], self.gz + gz)
        t = whole(self.sizes["ta"], self.ta + ta)
        if flip_gx:
            x = x + 1 - 2 * lax.rem(x, 2)
        if flip_ta & 1:
            t = t + 1 - 2 * lax.rem(t, 2)
        if flip_ta & 2:
            t = whole(self.sizes["ta"], t + 2)
        return {"gx": x, "gz": z, "ta": t}

    def ahead(self, direction, sign):
        if direction == 0:
            return self.at(gx=sign * self.row_len)
        if direction == 1:
            return self.at(gx=sign)
        if direction == 2:
            return self.at(gz=sign)
        return self.at(ta=sign)

    def stage(self, index):
        if index == 0:
            return [self.at(flip_ta=1)]
        if index == 1:
            turns = [(a, c, k) for k in (2, 1, 3, 0) for a in (1, 0) for c in (2, 0)]
            return [self.at(gz=k, flip_gx=a, flip_ta=c) for a, c, k in turns[:-1]]
        far = [16] + [sign * k for k in range(15, 0, -1) for sign in (1, -1)]
        return [self.at(gx=2 * k) for k in far]


def twice(values):
    return jnp.concatenate([values, values], axis=-1)


def turned(values):
    return pltpu.roll(values, 64, values.ndim - 1)


def groups():
    return [(x, y, z) for x in range(EXT[0]) for y in range(EXT[1]) for z in range(EXT[2])]


def signs():
    lane = lax.broadcasted_iota(jnp.int32, (1, 1, 128), 2)
    return jnp.where(lax.rem(lane, 64) < 32, 1.0, -1.0).astype(F32), lane < 64


def pack_links(hops, packed, pair):
    for g in groups():
        packed[g + (slice(None), slice(None), slice(128 * pair, 128 * pair + 128))] = jnp.concatenate(
            [hops[(2 * pair,) + g], hops[(2 * pair + 1,) + g]], axis=-1
        )


def local_apply(fields, outs, backs, links, packed, split, ahead_sum):
    chi, lower = signs()
    height = 16 * len(fields)
    rows = slice(0, height)
    for k, field in enumerate(fields):
        top = field[...].astype(BF16).astype(F32)
        split[..., 16 * k : 16 * k + 8, :] = top
        split[..., 16 * k + 8 : 16 * k + 16, :] = field[...] - top
    nil = jnp.zeros((4, height, 128), F32)
    for x, y, z in groups():
        own = split[x, y, z, :, rows, :]
        in_x = split[1, y, z, :, rows, :] if x == 0 else nil
        in_y = split[x, 1, z, :, rows, :] if y == 0 else nil
        in_z = split[x, y, z + 1, :, rows, :] if z < 3 else nil
        in_t = jnp.concatenate([own[1:], nil[:1]], axis=0)
        ahead = jnp.concatenate(
            [jnp.where(lower, in_x, in_y).astype(BF16), jnp.where(lower, in_z, in_t).astype(BF16)], axis=-1
        )
        onward = forward_dot(ahead, packed[x, y, z])
        onward = onward + forward_dot(own[..., :64].astype(BF16), links[x, y, z])
        back = backward_dot((own * chi)[..., :64].astype(BF16), packed[x, y, z])
        for k in range(len(fields)):
            a, b = slice(16 * k, 16 * k + 8), slice(16 * k + 8, 16 * k + 16)
            ahead_sum[x, y, z, :, 8 * k : 8 * k + 8, :] = onward[:, a] + onward[:, b]
            backs[k][x, y, z] = back[:, a] + back[:, b]
    nil = jnp.zeros((4, 8, 128), F32)
    for k, (field, out) in enumerate(zip(fields, outs)):
        for x, y, z in groups():
            first, second = slice(0, 128), slice(128, 256)
            in_x = backs[k][0, y, z, :, :, first] if x else nil
            in_y = backs[k][x, 0, z, :, :, first] if y else nil
            in_z = backs[k][x, y, z - 1, :, :, second] if z else nil
            in_t = jnp.concatenate([nil[:1], backs[k][x, y, z, 0:3, :, second]], axis=0)
            total = chi * (jnp.where(lower, in_x, in_y) + jnp.where(lower, in_z, in_t))
            onward = ahead_sum[x, y, z, :, 8 * k : 8 * k + 8, :]
            total = total + jnp.concatenate([onward, jnp.zeros_like(onward)], axis=-1)
            out[x, y, z] = 4.0 * field[x, y, z] + (total + turned(total))


def on_device(sizes, row_len, rhs_hbm, self_hbm, hop_hbm, sol_ref, res_ref,
              rhs_in, links, hops, packed, split, ahead_sum, back_a, back_b, back_c, back_d, halo_in,
              rhs, m0, m1, r1, d0, z_field, rt, lt, lz, lt2, lz2, d1,
              send_xy, send_zt, got_xy, got_zt, rows_out, rows_in,
              load_sem, halo_send, halo_recv, sum_send, sum_recv):
    place = Place(sizes, row_len)
    loads = [pltpu.make_async_copy(rhs_hbm, rhs_in, load_sem.at[0])]
    for d in range(4):
        loads.append(pltpu.make_async_copy(hop_hbm.at[d], hops.at[d], load_sem.at[1 + d]))
    loads.append(pltpu.make_async_copy(self_hbm, links, load_sem.at[5]))
    for load in loads:
        load.start()

    greeted = [place.ahead(d, sign) for d in range(4) for sign in (1, -1)]
    for index in range(len(STAGES)):
        greeted += place.stage(index)
    barrier = pltpu.get_barrier_semaphore()
    for other in greeted:
        pl.semaphore_signal(barrier, inc=1, device_id=other, device_id_type=MESH)

    chi, lower = signs()
    lane_r = lax.broadcasted_iota(jnp.int32, (8, 128), 1)
    sub_r = lax.broadcasted_iota(jnp.int32, (8, 128), 0)

    def dot_sum(a, b):
        summed = jnp.sum(flat(a[...]) * flat(b[...]), axis=0)
        return jnp.sum(summed[:, :64], axis=-1, keepdims=True)

    def to_row(columns):
        spread = jnp.zeros((8, 128), F32)
        for k, column in enumerate(columns):
            spread = jnp.where(lane_r == 8 * k + sub_r, column, spread)
        return jnp.sum(spread, axis=0, keepdims=True)

    def from_row(row, k):
        return jnp.sum(jnp.where(lane_r == 8 * k + sub_r, row, 0.0), axis=1, keepdims=True)

    def apply(fields, outs, backs):
        local_apply(fields, outs, backs, links, packed, split, ahead_sum)

    def face_ref(store, around, d, kind):
        xy, zt = store
        return (xy if d < 2 else zt).at[around, d % 2, kind]

    def halo_copy(around, d, kind):
        slot = (around * 4 + d) * 2 + kind
        return pltpu.make_async_remote_copy(
            src_ref=face_ref((send_xy, send_zt), around, d, kind),
            dst_ref=face_ref((got_xy, got_zt), around, d, kind),
            send_sem=halo_send.at[slot],
            recv_sem=halo_recv.at[slot],
            device_id=place.ahead(d, -1 if kind == 0 else 1),
            device_id_type=MESH,
        )

    def halo_start(around, field, back_of):
        for d in range(4):
            low = flat(field[part(d, 0, 1)])
            half = low.shape[0] // 2
            face_ref((send_xy, send_zt), around, d, 0)[...] = jnp.where(lower, low[:half], low[half:]).astype(BF16)
            halo_copy(around, d, 0).start()
            lanes = slice(128 * (d // 2), 128 * (d // 2) + 128)
            back = flat(chi * back_of(part(d, EXT[d] - 1, EXT[d]) + (slice(None), lanes)))
            if d % 2:
                back = jnp.where(lower, turned(back[:half]), back[half:])
            else:
                back = jnp.where(lower, back[:half], turned(back[half:]))
            face_ref((send_xy, send_zt), around, d, 1)[...] = back.astype(BF16)
            halo_copy(around, d, 1).start()

    def halo_finish(around, out):
        for d in (2, 3, 1, 0):
            shape = tuple(1 if k == d else EXT[k] for k in range(4)) + (8, 128)
            halo_copy(around, d, 0).wait_recv()
            got = face_ref((got_xy, got_zt), around, d, 0)[...].astype(F32)
            pieces = (turned(got), got) if d % 2 else (got, turned(got))
            lanes = slice(64 * (d % 2), 64 * (d % 2) + 64)
            place_in = slice(64 * d, 64 * d + 64)
            field = jnp.concatenate(pieces, axis=0).reshape(shape)[..., lanes]
            halo_in[part(d, EXT[d] - 1, EXT[d]) + (slice(None), place_in)] = field
            halo_copy(around, d, 1).wait_recv()
            got = face_ref((got_xy, got_zt), around, d, 1)[...].astype(F32)
            other = turned(got)
            both = jnp.concatenate([jnp.where(lower, got, other), jnp.where(lower, other, got)], axis=0)
            out[part(d, 0, 1)] += both.reshape(shape)
        for g in groups():
            onward = forward_dot(halo_in[g].astype(BF16), packed[g])
            out[g] += twice(onward)

    def sum_copies(around, index):
        base = around * SLOTS + sum(STAGES[:index])
        return [
            pltpu.make_async_remote_copy(
                src_ref=rows_out.at[around * 4 + index],
                dst_ref=rows_in.at[base + k],
                send_sem=sum_send.at[base + k],
                recv_sem=sum_recv.at[base + k],
                device_id=other,
                device_id_type=MESH,
            )
            for k, other in enumerate(place.stage(index))
        ]

    def mesh_sum(around, row, meanwhile=None):
        for index in range(len(STAGES)):
            base = around * SLOTS + sum(STAGES[:index])
            rows_out[around * 4 + index] = row
            copies = sum_copies(around, index)
            for copy in copies:
                copy.start()
            if index == len(STAGES) - 1 and meanwhile is not None:
                meanwhile()
            for copy in copies:
                copy.wait_recv()
            row = row + jnp.sum(rows_in[base : base + len(copies)], axis=0)
        return row

    halo_in[...] = jnp.zeros_like(halo_in)
    loads[0].wait()
    rhs[...] = twice(rhs_in[...])
    for pair in range(2):
        loads[1 + 2 * pair].wait()
        loads[2 + 2 * pair].wait()
        pack_links(hops, packed, pair)
    loads[5].wait()
    apply([rhs], [m0], [back_a])
    weight_a = dot_sum(m0, rhs) / dot_sum(m0, m0)
    r1[...] = rhs[...] - weight_a * m0[...]
    apply([r1], [m1], [back_b])
    weight_b = dot_sum(m1, r1) / dot_sum(m1, m1)
    d0[...] = weight_a * rhs[...] + weight_b * r1[...]
    pl.semaphore_wait(barrier, len(greeted))
    halo_start(0, d0, lambda at: weight_a * back_a[at] + weight_b * back_b[at])
    z_field[...] = weight_a * m0[...] + weight_b * m1[...]
    halo_finish(0, z_field)

    part_zr, part_zz = dot_sum(z_field, rhs), dot_sum(z_field, z_field)
    centre = jnp.where(part_zz > 0.0, part_zr / jnp.where(part_zz > 0.0, part_zz, 1.0), 0.0)

    def meanwhile():
        rt[...] = rhs[...] - centre * z_field[...]
        apply([rt, z_field], [lt, lz], [back_a, back_b])
        apply([lt, lz], [lt2, lz2], [back_c, back_d])

    sums = mesh_sum(0, to_row([part_zr, part_zz]), meanwhile)
    sum_zz = from_row(sums, 1)
    alpha = from_row(sums, 0) / sum_zz
    shift = alpha - centre
    r1[...] = rhs[...] - alpha * z_field[...]
    m0[...] = lt[...] - shift * lz[...]
    weight_a = dot_sum(m0, r1) / dot_sum(m0, m0)
    m1[...] = m0[...] - weight_a * (lt2[...] - shift * lz2[...])
    rt[...] = r1[...] - weight_a * m0[...]
    weight_b = dot_sum(m1, rt) / dot_sum(m1, m1)
    d1[...] = weight_a * r1[...] + weight_b * rt[...]
    near = weight_a + weight_b
    deep = weight_a * weight_b

    def back_of(at):
        return near * (back_a[at] - shift * back_b[at]) - deep * (back_c[at] - shift * back_d[at])

    halo_start(1, d1, back_of)
    lz[...] = weight_a * m0[...] + weight_b * m1[...]
    halo_finish(1, lz)

    columns = [dot_sum(z_field, lz), dot_sum(lz, r1), dot_sum(lz, lz), dot_sum(z_field, r1)]
    sums = mesh_sum(1, to_row(columns))
    cross, onto, square, kept = [from_row(sums, k) for k in range(4)]
    beta = cross / sum_zz
    alpha_b = (onto - beta * kept) / (square - beta * (2.0 * cross - beta * sum_zz))
    sol_ref[...] = (alpha * d0[...] + alpha_b * (d1[...] - beta * d0[...]))[..., :64]
    res_ref[...] = (r1[...] - alpha_b * (lz[...] - beta * z_field[...]))[..., :64]

    for around in range(2):
        for d in range(4):
            for kind in range(2):
                halo_copy(around, d, kind).wait_send()
        for index in range(len(STAGES)):
            for copy in sum_copies(around, index):
                copy.wait_send()


def solution(mesh):
    sizes = dict(mesh.shape)
    row_len = min(8, max(2, sizes["gx"] // 8))

    def step(rhs, self_coupling, hopping):
        field = EXT + (8, 64)
        vmem = pl.BlockSpec(memory_space=pltpu.VMEM)
        hbm = pl.BlockSpec(memory_space=pl.ANY)
        fields = [pltpu.VMEM(EXT + (8, 128), F32)] * 12
        backs = [pltpu.VMEM(EXT + (8, 256), F32)] * 5
        sol, res = pl.pallas_call(
            functools.partial(on_device, sizes, row_len),
            out_shape=[jax.ShapeDtypeStruct(field, F32)] * 2,
            in_specs=[hbm] * 3,
            out_specs=[vmem] * 2,
            scratch_shapes=[
                pltpu.VMEM(field, F32),
                pltpu.VMEM(EXT + (64, 64), BF16),
                pltpu.VMEM((4,) + EXT + (64, 64), BF16),
                pltpu.VMEM(EXT + (64, 256), BF16),
                pltpu.VMEM(EXT + (32, 128), F32),
                pltpu.VMEM(EXT + (16, 64), F32),
                *backs,
                *fields,
                pltpu.VMEM((2, 2, 2, 16, 8, 128), BF16),
                pltpu.VMEM((2, 2, 2, 8, 8, 128), BF16),
                pltpu.VMEM((2, 2, 2, 16, 8, 128), BF16),
                pltpu.VMEM((2, 2, 2, 8, 8, 128), BF16),
                pltpu.VMEM((8, 1, 128), F32),
                pltpu.VMEM((2 * SLOTS, 1, 128), F32),
                pltpu.SemaphoreType.DMA((6,)),
                pltpu.SemaphoreType.DMA((16,)),
                pltpu.SemaphoreType.DMA((16,)),
                pltpu.SemaphoreType.DMA((2 * SLOTS,)),
                pltpu.SemaphoreType.DMA((2 * SLOTS,)),
            ],
            compiler_params=pltpu.CompilerParams(collective_id=0, has_side_effects=True),
        )(rhs[0], self_coupling[0], hopping[:, 0])
        return sol[None], res[None]

    whole_spec = P("gx", None, None, "gz", "ta", None, None)
    return jax.shard_map(
        step,
        mesh=mesh,
        in_specs=(whole_spec, whole_spec, P(None, "gx", None, None, "gz", "ta", None, None)),
        out_specs=(whole_spec, whole_spec),
        check_vma=False,
    )
```

```python
import functools

import jax
import jax.numpy as jnp
from jax import lax
from jax.experimental import pallas as pl
from jax.experimental.pallas import tpu as pltpu
from jax.sharding import PartitionSpec as P

MESH = pl.DeviceIdType.MESH
EXT = (2, 2, 4, 4)
F32 = jnp.float32
BF16 = jnp.bfloat16
STAGES = (1, 15, 31)
SLOTS = sum(STAGES)


def part(direction, low, high):
    return tuple(slice(low, high) if d == direction else slice(None) for d in range(4))


def flat(values):
    return values.reshape((-1,) + values.shape[4:])


def forward_dot(fields, links):
    return lax.dot_general(fields, links, (((2,), (2,)), ((0,), (0,))), preferred_element_type=F32)


def backward_dot(fields, links):
    return lax.dot_general(fields, links, (((2,), (1,)), ((0,), (0,))), preferred_element_type=F32)


def whole(mesh_size, value):
    return lax.rem(value + mesh_size, mesh_size)


class Place:
    def __init__(self, sizes, row_len):
        self.sizes = sizes
        self.row_len = row_len
        self.gx = lax.axis_index("gx")
        self.gz = lax.axis_index("gz")
        self.ta = lax.axis_index("ta")

    def at(self, gx=0, gz=0, ta=0, flip_gx=0, flip_ta=0):
        x = whole(self.sizes["gx"], self.gx + gx)
        z = whole(self.sizes["gz"], self.gz + gz)
        t = whole(self.sizes["ta"], self.ta + ta)
        if flip_gx:
            x = x + 1 - 2 * lax.rem(x, 2)
        if flip_ta & 1:
            t = t + 1 - 2 * lax.rem(t, 2)
        if flip_ta & 2:
            t = whole(self.sizes["ta"], t + 2)
        return {"gx": x, "gz": z, "ta": t}

    def ahead(self, direction, sign):
        if direction == 0:
            return self.at(gx=sign * self.row_len)
        if direction == 1:
            return self.at(gx=sign)
        if direction == 2:
            return self.at(gz=sign)
        return self.at(ta=sign)

    def stage(self, index):
        if index == 0:
            return [self.at(flip_ta=1)]
        if index == 1:
            turns = [(a, c, k) for k in (2, 1, 3, 0) for a in (1, 0) for c in (2, 0)]
            return [self.at(gz=k, flip_gx=a, flip_ta=c) for a, c, k in turns[:-1]]
        far = [16] + [sign * k for k in range(15, 0, -1) for sign in (1, -1)]
        return [self.at(gx=2 * k) for k in far]


def twice(values):
    return jnp.concatenate([values, values], axis=-1)


def turned(values):
    return pltpu.roll(values, 64, values.ndim - 1)


def groups():
    return [(x, y, z) for x in range(EXT[0]) for y in range(EXT[1]) for z in range(EXT[2])]


def signs():
    lane = lax.broadcasted_iota(jnp.int32, (1, 1, 128), 2)
    return jnp.where(lax.rem(lane, 64) < 32, 1.0, -1.0).astype(F32), lane < 64


def pack_links(hops, packed, pair):
    for g in groups():
        packed[g + (slice(None), slice(None), slice(128 * pair, 128 * pair + 128))] = jnp.concatenate(
            [hops[(2 * pair,) + g], hops[(2 * pair + 1,) + g]], axis=-1
        )


def local_apply(fields, outs, backs, links, packed, split, ahead_sum):
    chi, lower = signs()
    height = 16 * len(fields)
    rows = slice(0, height)
    for k, field in enumerate(fields):
        top = field[...].astype(BF16).astype(F32)
        split[..., 16 * k : 16 * k + 8, :] = top
        split[..., 16 * k + 8 : 16 * k + 16, :] = field[...] - top
    nil = jnp.zeros((4, height, 128), F32)
    for x, y, z in groups():
        own = split[x, y, z, :, rows, :]
        in_x = split[1, y, z, :, rows, :] if x == 0 else nil
        in_y = split[x, 1, z, :, rows, :] if y == 0 else nil
        in_z = split[x, y, z + 1, :, rows, :] if z < 3 else nil
        in_t = jnp.concatenate([own[1:], nil[:1]], axis=0)
        ahead = jnp.concatenate(
            [jnp.where(lower, in_x, in_y).astype(BF16), jnp.where(lower, in_z, in_t).astype(BF16)], axis=-1
        )
        onward = forward_dot(ahead, packed[x, y, z])
        onward = onward + forward_dot(own[..., :64].astype(BF16), links[x, y, z])
        back = backward_dot((own * chi)[..., :64].astype(BF16), packed[x, y, z])
        for k in range(len(fields)):
            a, b = slice(16 * k, 16 * k + 8), slice(16 * k + 8, 16 * k + 16)
            ahead_sum[x, y, z, :, 8 * k : 8 * k + 8, :] = onward[:, a] + onward[:, b]
            backs[k][x, y, z] = back[:, a] + back[:, b]
    nil = jnp.zeros((4, 8, 128), F32)
    for k, (field, out) in enumerate(zip(fields, outs)):
        for x, y, z in groups():
            first, second = slice(0, 128), slice(128, 256)
            in_x = backs[k][0, y, z, :, :, first] if x else nil
            in_y = backs[k][x, 0, z, :, :, first] if y else nil
            in_z = backs[k][x, y, z - 1, :, :, second] if z else nil
            in_t = jnp.concatenate([nil[:1], backs[k][x, y, z, 0:3, :, second]], axis=0)
            total = chi * (jnp.where(lower, in_x, in_y) + jnp.where(lower, in_z, in_t))
            onward = ahead_sum[x, y, z, :, 8 * k : 8 * k + 8, :]
            total = total + jnp.concatenate([onward, jnp.zeros_like(onward)], axis=-1)
            out[x, y, z] = 4.0 * field[x, y, z] + (total + turned(total))


def on_device(sizes, row_len, rhs_hbm, self_hbm, hop_hbm, pair_out, zero_out, left_out, scale_out,
              rhs_in, links, hops, packed, split, ahead_sum, back_a, back_b, back_c, back_d, halo_in,
              rhs, m0, n0, m1, r1, d0, z_field, rt, lt, lz, lt2, lz2, d1, raw, left,
              send_xy, send_zt, got_xy, got_zt, rows_out, rows_in, gram_out, gram_in,
              load_sem, halo_send, halo_recv, sum_send, sum_recv, gram_send, gram_recv):
    place = Place(sizes, row_len)
    loads = [pltpu.make_async_copy(rhs_hbm, rhs_in, load_sem.at[0])]
    for d in range(4):
        loads.append(pltpu.make_async_copy(hop_hbm.at[d], hops.at[d], load_sem.at[1 + d]))
    loads.append(pltpu.make_async_copy(self_hbm, links, load_sem.at[5]))
    for load in loads:
        load.start()

    greeted = [place.ahead(d, sign) for d in range(4) for sign in (1, -1)]
    for index in range(len(STAGES)):
        greeted += place.stage(index)
    barrier = pltpu.get_barrier_semaphore()
    for other in greeted:
        pl.semaphore_signal(barrier, inc=1, device_id=other, device_id_type=MESH)

    chi, lower = signs()
    lane_r = lax.broadcasted_iota(jnp.int32, (8, 128), 1)
    sub_r = lax.broadcasted_iota(jnp.int32, (8, 128), 0)

    def dot_sum(a, b):
        summed = jnp.sum(flat(a[...]) * flat(b[...]), axis=0)
        return jnp.sum(summed[:, :64], axis=-1, keepdims=True)

    def to_row(columns):
        spread = jnp.zeros((8, 128), F32)
        for k, column in enumerate(columns):
            spread = jnp.where(lane_r == 8 * k + sub_r, column, spread)
        return jnp.sum(spread, axis=0, keepdims=True)

    def from_row(row, k):
        return jnp.sum(jnp.where(lane_r == 8 * k + sub_r, row, 0.0), axis=1, keepdims=True)

    def apply(fields, outs, backs):
        local_apply(fields, outs, backs, links, packed, split, ahead_sum)

    def face_ref(store, around, d, kind):
        xy, zt = store
        return (xy if d < 2 else zt).at[around, d % 2, kind]

    def halo_copy(around, d, kind):
        slot = (around * 4 + d) * 2 + kind
        return pltpu.make_async_remote_copy(
            src_ref=face_ref((send_xy, send_zt), around, d, kind),
            dst_ref=face_ref((got_xy, got_zt), around, d, kind),
            send_sem=halo_send.at[slot],
            recv_sem=halo_recv.at[slot],
            device_id=place.ahead(d, -1 if kind == 0 else 1),
            device_id_type=MESH,
        )

    def send_fields(around, field):
        for d in range(4):
            low = flat(field[part(d, 0, 1)])
            half = low.shape[0] // 2
            face_ref((send_xy, send_zt), around, d, 0)[...] = jnp.where(lower, low[:half], low[half:]).astype(BF16)
            halo_copy(around, d, 0).start()

    def send_backs(around, back_of):
        for d in range(4):
            lanes = slice(128 * (d // 2), 128 * (d // 2) + 128)
            back = flat(chi * back_of(part(d, EXT[d] - 1, EXT[d]) + (slice(None), lanes)))
            half = back.shape[0] // 2
            if d % 2:
                back = jnp.where(lower, turned(back[:half]), back[half:])
            else:
                back = jnp.where(lower, back[:half], turned(back[half:]))
            face_ref((send_xy, send_zt), around, d, 1)[...] = back.astype(BF16)
            halo_copy(around, d, 1).start()

    def received(around, d, kind):
        halo_copy(around, d, kind).wait_recv()
        return face_ref((got_xy, got_zt), around, d, kind)[...].astype(F32)

    def halo_finish(out, face):
        for d in (2, 3, 1, 0):
            shape = tuple(1 if k == d else EXT[k] for k in range(4)) + (8, 128)
            got = face(d, 0)
            pieces = (turned(got), got) if d % 2 else (got, turned(got))
            lanes = slice(64 * (d % 2), 64 * (d % 2) + 64)
            place_in = slice(64 * d, 64 * d + 64)
            field = jnp.concatenate(pieces, axis=0).reshape(shape)[..., lanes]
            halo_in[part(d, EXT[d] - 1, EXT[d]) + (slice(None), place_in)] = field
            got = face(d, 1)
            other = turned(got)
            both = jnp.concatenate([jnp.where(lower, got, other), jnp.where(lower, other, got)], axis=0)
            out[part(d, 0, 1)] += both.reshape(shape)
        for g in groups():
            onward = forward_dot(halo_in[g].astype(BF16), packed[g])
            out[g] += twice(onward)

    def gram_copies():
        return [
            pltpu.make_async_remote_copy(
                src_ref=gram_out.at[0],
                dst_ref=gram_in.at[2 * d + kind],
                send_sem=gram_send.at[2 * d + kind],
                recv_sem=gram_recv.at[2 * d + kind],
                device_id=place.ahead(d, -1 if kind == 0 else 1),
                device_id_type=MESH,
            )
            for d in range(4)
            for kind in range(2)
        ]

    def neighbour_weights(columns, alpha):
        shift = alpha - columns[0]
        onto, square, deep_onto, deep_cross, deep_square = [
            columns[k] - shift * (columns[k + 1] - shift * columns[k + 2]) for k in (1, 4, 7, 10, 13)
        ]
        first = onto / square
        top = onto - first * square - first * (deep_onto - first * deep_cross)
        second = top / (square - first * (2.0 * deep_cross - first * deep_square))
        return first + second, first * second

    def sum_copies(around, index):
        base = around * SLOTS + sum(STAGES[:index])
        return [
            pltpu.make_async_remote_copy(
                src_ref=rows_out.at[around * 4 + index],
                dst_ref=rows_in.at[base + k],
                send_sem=sum_send.at[base + k],
                recv_sem=sum_recv.at[base + k],
                device_id=other,
                device_id_type=MESH,
            )
            for k, other in enumerate(place.stage(index))
        ]

    def mesh_sum(around, row, meanwhile=(None, None, None)):
        for index in range(len(STAGES)):
            base = around * SLOTS + sum(STAGES[:index])
            rows_out[around * 4 + index] = row
            copies = sum_copies(around, index)
            for copy in copies:
                copy.start()
            if meanwhile[index] is not None:
                meanwhile[index]()
            for copy in copies:
                copy.wait_recv()
            row = row + jnp.sum(rows_in[base : base + len(copies)], axis=0)
        return row

    halo_in[...] = jnp.zeros_like(halo_in)
    loads[0].wait()
    rhs[...] = twice(rhs_in[...])
    for pair in range(2):
        loads[1 + 2 * pair].wait()
        loads[2 + 2 * pair].wait()
        pack_links(hops, packed, pair)
    loads[5].wait()
    apply([rhs], [m0], [back_a])
    apply([m0], [n0], [back_b])
    weight_a = dot_sum(m0, rhs) / dot_sum(m0, m0)
    r1[...] = rhs[...] - weight_a * m0[...]
    m1[...] = m0[...] - weight_a * n0[...]
    weight_b = dot_sum(m1, r1) / dot_sum(m1, m1)
    near, deep = weight_a + weight_b, weight_a * weight_b
    d0[...] = weight_a * rhs[...] + weight_b * r1[...]
    pl.semaphore_wait(barrier, len(greeted))
    send_fields(0, d0)
    send_backs(0, lambda at: near * back_a[at] - deep * back_b[at])
    send_fields(1, rhs)
    send_backs(1, lambda at: back_a[at])
    send_fields(2, m0)
    send_backs(2, lambda at: back_b[at])
    z_field[...] = weight_a * m0[...] + weight_b * m1[...]
    halo_finish(z_field, lambda d, kind: received(0, d, kind))

    part_zr, part_zz = dot_sum(z_field, rhs), dot_sum(z_field, z_field)
    columns_in = []

    def in_core_stage():
        send_fields(3, z_field)

    def in_plane_stage():
        apply([z_field], [lz], [back_c])
        send_backs(3, lambda at: back_c[at])
        send_fields(4, lz)
        apply([lz], [lz2], [back_d])
        send_backs(4, lambda at: back_d[at])

    def in_column_stage():
        centre = jnp.where(part_zz > 0.0, part_zr / jnp.where(part_zz > 0.0, part_zz, 1.0), 0.0)
        rt[...] = rhs[...] - centre * z_field[...]
        lt[...] = m0[...] - centre * lz[...]
        lt2[...] = n0[...] - centre * lz2[...]
        gram = [
            centre,
            dot_sum(lt, rt), dot_sum(lt, z_field) + dot_sum(lz, rt), dot_sum(lz, z_field),
            dot_sum(lt, lt), 2.0 * dot_sum(lt, lz), dot_sum(lz, lz),
            dot_sum(lt2, rt), dot_sum(lt2, z_field) + dot_sum(lz2, rt), dot_sum(lz2, z_field),
            dot_sum(lt2, lt), dot_sum(lt2, lz) + dot_sum(lz2, lt), dot_sum(lz2, lz),
            dot_sum(lt2, lt2), 2.0 * dot_sum(lt2, lz2), dot_sum(lz2, lz2),
        ]
        gram_out[0] = to_row(gram)
        copies = gram_copies()
        for copy in copies:
            copy.start()
        near, deep = neighbour_weights(gram, centre)
        d1[...] = near * rt[...] - deep * lt[...]
        send_fields(5, d1)
        send_backs(
            5,
            lambda at: near * (back_a[at] - centre * back_c[at]) - deep * (back_b[at] - centre * back_d[at]),
        )
        for k, copy in enumerate(copies):
            copy.wait_recv()
            row = gram_in[k]
            columns = [from_row(row, c) for c in range(16)]
            columns_in.append((columns, neighbour_weights(columns, columns[0])))

    sums = mesh_sum(0, to_row([part_zr, part_zz]), (in_core_stage, in_plane_stage, in_column_stage))
    sum_zz = from_row(sums, 1)
    alpha = from_row(sums, 0) / sum_zz
    r1[...] = rhs[...] - alpha * z_field[...]
    lt[...] = m0[...] - alpha * lz[...]
    weight_a = dot_sum(lt, r1) / dot_sum(lt, lt)
    m1[...] = lt[...] - weight_a * (n0[...] - alpha * lz2[...])
    left[...] = r1[...] - weight_a * lt[...]
    weight_b = dot_sum(m1, left) / dot_sum(m1, m1)
    d1[...] = weight_a * r1[...] + weight_b * left[...]
    raw[...] = weight_a * lt[...] + weight_b * m1[...]

    def face(d, kind):
        columns, (near_mid, deep_mid) = columns_in[2 * d + kind]
        near, deep = neighbour_weights(columns, alpha)
        source, mapped, zero, again, middle = [received(around, d, kind) for around in range(1, 6)]
        centre, shift = columns[0], alpha - columns[0]
        more, less = near - near_mid, deep - deep_mid
        return (middle + more * source - less * mapped - (more * centre + near * shift) * zero
                + (less * centre + deep * shift) * again)

    halo_finish(raw, face)

    columns = [dot_sum(z_field, raw), dot_sum(raw, r1), dot_sum(raw, raw), dot_sum(z_field, r1)]
    outs = [pltpu.make_async_copy(source, place_out, load_sem.at[k])
            for k, (source, place_out) in enumerate(((rt, pair_out), (lt2, zero_out), (r1, left_out)))]

    def in_last_stage():
        rt[...] = jnp.where(lower, d0[...], d1[...])
        lt2[...] = jnp.where(lower, z_field[...], raw[...])
        for out in outs:
            out.start()

    sums = mesh_sum(1, to_row(columns), (None, None, in_last_stage))
    cross, onto, square, kept = [from_row(sums, k) for k in range(4)]
    beta = cross / sum_zz
    alpha_b = (onto - beta * kept) / (square - beta * (2.0 * cross - beta * sum_zz))
    half = lane_r < 64
    scale_out[0] = jnp.where(half, alpha - alpha_b * beta, alpha_b)
    scale_out[1] = jnp.where(half, alpha_b * beta, -alpha_b)

    for out in outs:
        out.wait()
    for around in range(6):
        for d in range(4):
            for kind in range(2):
                halo_copy(around, d, kind).wait_send()
    for copy in gram_copies():
        copy.wait_send()
    for around in range(2):
        for index in range(len(STAGES)):
            for copy in sum_copies(around, index):
                copy.wait_send()


def combine(pair_ref, zero_ref, left_ref, scale_ref, sol_ref, res_ref):
    first = scale_ref[0] * pair_ref[...]
    second = scale_ref[1] * zero_ref[...]
    sol_ref[...] = (first + turned(first))[..., :64]
    res_ref[...] = (left_ref[...] + (second + turned(second)))[..., :64]


def solution(mesh):
    sizes = dict(mesh.shape)
    row_len = min(8, max(2, sizes["gx"] // 8))

    def step(rhs, self_coupling, hopping):
        field = EXT + (8, 64)
        vmem = pl.BlockSpec(memory_space=pltpu.VMEM)
        hbm = pl.BlockSpec(memory_space=pl.ANY)
        fields = [pltpu.VMEM(EXT + (8, 128), F32)] * 15
        backs = [pltpu.VMEM(EXT + (8, 256), F32)] * 5
        parts = pl.pallas_call(
            functools.partial(on_device, sizes, row_len),
            out_shape=[jax.ShapeDtypeStruct(EXT + (8, 128), F32)] * 3 + [jax.ShapeDtypeStruct((2, 8, 128), F32)],
            in_specs=[hbm] * 3,
            out_specs=[hbm] * 3 + [vmem],
            scratch_shapes=[
                pltpu.VMEM(field, F32),
                pltpu.VMEM(EXT + (64, 64), BF16),
                pltpu.VMEM((4,) + EXT + (64, 64), BF16),
                pltpu.VMEM(EXT + (64, 256), BF16),
                pltpu.VMEM(EXT + (16, 128), F32),
                pltpu.VMEM(EXT + (8, 64), F32),
                *backs,
                *fields,
                pltpu.VMEM((6, 2, 2, 16, 8, 128), BF16),
                pltpu.VMEM((6, 2, 2, 8, 8, 128), BF16),
                pltpu.VMEM((6, 2, 2, 16, 8, 128), BF16),
                pltpu.VMEM((6, 2, 2, 8, 8, 128), BF16),
                pltpu.VMEM((8, 1, 128), F32),
                pltpu.VMEM((2 * SLOTS, 1, 128), F32),
                pltpu.VMEM((1, 1, 128), F32),
                pltpu.VMEM((8, 1, 128), F32),
                pltpu.SemaphoreType.DMA((6,)),
                pltpu.SemaphoreType.DMA((48,)),
                pltpu.SemaphoreType.DMA((48,)),
                pltpu.SemaphoreType.DMA((2 * SLOTS,)),
                pltpu.SemaphoreType.DMA((2 * SLOTS,)),
                pltpu.SemaphoreType.DMA((8,)),
                pltpu.SemaphoreType.DMA((8,)),
            ],
            compiler_params=pltpu.CompilerParams(collective_id=0, has_side_effects=True),
        )(rhs[0], self_coupling[0], hopping[:, 0])
        sol, res = pl.pallas_call(
            combine,
            out_shape=[jax.ShapeDtypeStruct(field, F32)] * 2,
            in_specs=[vmem] * 4,
            out_specs=[vmem] * 2,
        )(*parts)
        return sol[None], res[None]

    whole_spec = P("gx", None, None, "gz", "ta", None, None)
    return jax.shard_map(
        step,
        mesh=mesh,
        in_specs=(whole_spec, whole_spec, P(None, "gx", None, None, "gz", "ta", None, None)),
        out_specs=(whole_spec, whole_spec),
        check_vma=False,
    )
```

```python
import functools

import jax
import jax.numpy as jnp
from jax import lax
from jax.experimental import pallas as pl
from jax.experimental.pallas import tpu as pltpu
from jax.sharding import PartitionSpec as P

MESH = pl.DeviceIdType.MESH
EXT = (2, 2, 4, 4)
F32 = jnp.float32
BF16 = jnp.bfloat16
STAGES = (15, 63)
SLOTS = sum(STAGES)


def part(direction, low, high):
    return tuple(slice(low, high) if d == direction else slice(None) for d in range(4))


def flat(values):
    return values.reshape((-1,) + values.shape[4:])


def forward_dot(fields, links):
    return lax.dot_general(fields, links, (((2,), (2,)), ((0,), (0,))), preferred_element_type=F32)


def backward_dot(fields, links):
    return lax.dot_general(fields, links, (((2,), (1,)), ((0,), (0,))), preferred_element_type=F32)


def whole(mesh_size, value):
    return lax.rem(value + mesh_size, mesh_size)


class Place:
    def __init__(self, sizes, row_len):
        self.sizes = sizes
        self.row_len = row_len
        self.gx = lax.axis_index("gx")
        self.gz = lax.axis_index("gz")
        self.ta = lax.axis_index("ta")

    def at(self, gx=0, gz=0, ta=0, flip_gx=0, flip_ta=0):
        x = whole(self.sizes["gx"], self.gx + gx)
        z = whole(self.sizes["gz"], self.gz + gz)
        t = whole(self.sizes["ta"], self.ta + ta)
        if flip_gx:
            x = x + 1 - 2 * lax.rem(x, 2)
        if flip_ta & 1:
            t = t + 1 - 2 * lax.rem(t, 2)
        if flip_ta & 2:
            t = whole(self.sizes["ta"], t + 2)
        return {"gx": x, "gz": z, "ta": t}

    def ahead(self, direction, sign):
        if direction == 0:
            return self.at(gx=sign * self.row_len)
        if direction == 1:
            return self.at(gx=sign)
        if direction == 2:
            return self.at(gz=sign)
        return self.at(ta=sign)

    def stage(self, index):
        if index == 0:
            turns = [(a, c, k) for k in (2, 1, 3, 0) for a in (1, 0) for c in (2, 0)]
            return [self.at(gz=k, flip_gx=a, flip_ta=c) for a, c, k in turns[:-1]]
        far = [16] + [sign * k for k in range(15, 0, -1) for sign in (1, -1)]
        return [self.at(gx=2 * k, flip_ta=c) for k in far for c in (0, 1)] + [self.at(flip_ta=1)]


def twice(values):
    return jnp.concatenate([values, values], axis=-1)


def turned(values):
    return pltpu.roll(values, 64, values.ndim - 1)


def groups():
    return [(x, y, z) for x in range(EXT[0]) for y in range(EXT[1]) for z in range(EXT[2])]


def signs():
    lane = lax.broadcasted_iota(jnp.int32, (1, 1, 128), 2)
    return jnp.where(lax.rem(lane, 64) < 32, 1.0, -1.0).astype(F32), lane < 64


def pack_links(hops, packed, pair):
    for g in groups():
        packed[g + (slice(None), slice(None), slice(128 * pair, 128 * pair + 128))] = jnp.concatenate(
            [hops[(2 * pair,) + g], hops[(2 * pair + 1,) + g]], axis=-1
        )


def local_apply(fields, outs, backs, links, packed, split, ahead_sum):
    chi, lower = signs()
    height = 16 * len(fields)
    rows = slice(0, height)
    for k, field in enumerate(fields):
        top = field[...].astype(BF16).astype(F32)
        split[..., 16 * k : 16 * k + 8, :] = top
        split[..., 16 * k + 8 : 16 * k + 16, :] = field[...] - top
    nil = jnp.zeros((4, height, 128), F32)
    for x, y, z in groups():
        own = split[x, y, z, :, rows, :]
        in_x = split[1, y, z, :, rows, :] if x == 0 else nil
        in_y = split[x, 1, z, :, rows, :] if y == 0 else nil
        in_z = split[x, y, z + 1, :, rows, :] if z < 3 else nil
        in_t = jnp.concatenate([own[1:], nil[:1]], axis=0)
        ahead = jnp.concatenate(
            [jnp.where(lower, in_x, in_y).astype(BF16), jnp.where(lower, in_z, in_t).astype(BF16)], axis=-1
        )
        onward = forward_dot(ahead, packed[x, y, z])
        onward = onward + forward_dot(own[..., :64].astype(BF16), links[x, y, z])
        back = backward_dot((own * chi)[..., :64].astype(BF16), packed[x, y, z])
        for k in range(len(fields)):
            a, b = slice(16 * k, 16 * k + 8), slice(16 * k + 8, 16 * k + 16)
            ahead_sum[x, y, z, :, 8 * k : 8 * k + 8, :] = onward[:, a] + onward[:, b]
            backs[k][x, y, z] = back[:, a] + back[:, b]
    nil = jnp.zeros((4, 8, 128), F32)
    for k, (field, out) in enumerate(zip(fields, outs)):
        for x, y, z in groups():
            first, second = slice(0, 128), slice(128, 256)
            in_x = backs[k][0, y, z, :, :, first] if x else nil
            in_y = backs[k][x, 0, z, :, :, first] if y else nil
            in_z = backs[k][x, y, z - 1, :, :, second] if z else nil
            in_t = jnp.concatenate([nil[:1], backs[k][x, y, z, 0:3, :, second]], axis=0)
            total = chi * (jnp.where(lower, in_x, in_y) + jnp.where(lower, in_z, in_t))
            onward = ahead_sum[x, y, z, :, 8 * k : 8 * k + 8, :]
            total = total + jnp.concatenate([onward, jnp.zeros_like(onward)], axis=-1)
            out[x, y, z] = 4.0 * field[x, y, z] + (total + turned(total))


def on_device(sizes, row_len, rhs_hbm, self_hbm, hop_hbm, pair_out, zero_out, left_out, scale_out,
              rhs_in, links, hops, packed, split, ahead_sum, back_a, back_b, back_c, back_d, halo_in,
              rhs, m0, n0, m1, r1, d0, z_field, rt, lt, lz, lt2, lz2, d1, raw,
              send_xy, send_zt, got_xy, got_zt, rows_out, rows_in,
              load_sem, halo_send, halo_recv, sum_send, sum_recv):
    place = Place(sizes, row_len)
    loads = [pltpu.make_async_copy(rhs_hbm, rhs_in, load_sem.at[0])]
    for d in range(4):
        loads.append(pltpu.make_async_copy(hop_hbm.at[d], hops.at[d], load_sem.at[1 + d]))
    loads.append(pltpu.make_async_copy(self_hbm, links, load_sem.at[5]))
    for load in loads:
        load.start()

    greeted = [place.ahead(d, sign) for d in range(4) for sign in (1, -1)]
    for index in range(len(STAGES)):
        greeted += place.stage(index)
    barrier = pltpu.get_barrier_semaphore()
    for other in greeted:
        pl.semaphore_signal(barrier, inc=1, device_id=other, device_id_type=MESH)

    chi, lower = signs()
    lane_r = lax.broadcasted_iota(jnp.int32, (8, 128), 1)
    sub_r = lax.broadcasted_iota(jnp.int32, (8, 128), 0)

    def dot_sum(a, b):
        summed = jnp.sum(flat(a[...]) * flat(b[...]), axis=0)
        return jnp.sum(summed[:, :64], axis=-1, keepdims=True)

    def to_row(columns):
        spread = jnp.zeros((8, 128), F32)
        for k, column in enumerate(columns):
            spread = jnp.where(lane_r == 8 * k + sub_r, column, spread)
        return jnp.sum(spread, axis=0, keepdims=True)

    def from_row(row, k):
        return jnp.sum(jnp.where(lane_r == 8 * k + sub_r, row, 0.0), axis=1, keepdims=True)

    def apply(fields, outs, backs):
        local_apply(fields, outs, backs, links, packed, split, ahead_sum)

    def face_ref(store, around, d, kind):
        xy, zt = store
        return (xy if d < 2 else zt).at[around, d % 2, kind]

    def halo_copy(around, d, kind):
        slot = (around * 4 + d) * 2 + kind
        return pltpu.make_async_remote_copy(
            src_ref=face_ref((send_xy, send_zt), around, d, kind),
            dst_ref=face_ref((got_xy, got_zt), around, d, kind),
            send_sem=halo_send.at[slot],
            recv_sem=halo_recv.at[slot],
            device_id=place.ahead(d, -1 if kind == 0 else 1),
            device_id_type=MESH,
        )

    def send_fields(around, field):
        for d in range(4):
            low = flat(field[part(d, 0, 1)])
            half = low.shape[0] // 2
            face_ref((send_xy, send_zt), around, d, 0)[...] = jnp.where(lower, low[:half], low[half:]).astype(BF16)
            halo_copy(around, d, 0).start()

    def send_backs(around, back_of):
        for d in range(4):
            lanes = slice(128 * (d // 2), 128 * (d // 2) + 128)
            back = flat(chi * back_of(part(d, EXT[d] - 1, EXT[d]) + (slice(None), lanes)))
            half = back.shape[0] // 2
            if d % 2:
                back = jnp.where(lower, turned(back[:half]), back[half:])
            else:
                back = jnp.where(lower, back[:half], turned(back[half:]))
            face_ref((send_xy, send_zt), around, d, 1)[...] = back.astype(BF16)
            halo_copy(around, d, 1).start()

    def received(around, d, kind):
        halo_copy(around, d, kind).wait_recv()
        return face_ref((got_xy, got_zt), around, d, kind)[...].astype(F32)

    def halo_finish(out, face):
        for d in (2, 3, 1, 0):
            shape = tuple(1 if k == d else EXT[k] for k in range(4)) + (8, 128)
            got = face(d, 0)
            pieces = (turned(got), got) if d % 2 else (got, turned(got))
            lanes = slice(64 * (d % 2), 64 * (d % 2) + 64)
            place_in = slice(64 * d, 64 * d + 64)
            field = jnp.concatenate(pieces, axis=0).reshape(shape)[..., lanes]
            halo_in[part(d, EXT[d] - 1, EXT[d]) + (slice(None), place_in)] = field
            got = face(d, 1)
            other = turned(got)
            both = jnp.concatenate([jnp.where(lower, got, other), jnp.where(lower, other, got)], axis=0)
            out[part(d, 0, 1)] += both.reshape(shape)
        for g in groups():
            onward = forward_dot(halo_in[g].astype(BF16), packed[g])
            out[g] += twice(onward)

    def smoothing_weights(columns, alpha):
        shift = alpha - columns[0]
        onto, square, deep_onto, deep_cross, deep_square = [
            columns[k] - shift * (columns[k + 1] - shift * columns[k + 2]) for k in (1, 4, 7, 10, 13)
        ]
        first = onto / square
        top = onto - first * square - first * (deep_onto - first * deep_cross)
        second = top / (square - first * (2.0 * deep_cross - first * deep_square))
        return first + second, first * second

    def sum_copies(around, index):
        base = around * SLOTS + sum(STAGES[:index])
        return [
            pltpu.make_async_remote_copy(
                src_ref=rows_out.at[around * 4 + index],
                dst_ref=rows_in.at[base + k],
                send_sem=sum_send.at[base + k],
                recv_sem=sum_recv.at[base + k],
                device_id=other,
                device_id_type=MESH,
            )
            for k, other in enumerate(place.stage(index))
        ]

    def mesh_sum(around, row, meanwhile=(None, None)):
        for index in range(len(STAGES)):
            base = around * SLOTS + sum(STAGES[:index])
            rows_out[around * 4 + index] = row
            copies = sum_copies(around, index)
            for copy in copies:
                copy.start()
            if meanwhile[index] is not None:
                meanwhile[index]()
            for copy in copies:
                copy.wait_recv()
            row = row + jnp.sum(rows_in[base : base + len(copies)], axis=0)
        return row

    halo_in[...] = jnp.zeros_like(halo_in)
    loads[0].wait()
    rhs[...] = twice(rhs_in[...])
    for pair in range(2):
        loads[1 + 2 * pair].wait()
        loads[2 + 2 * pair].wait()
        pack_links(hops, packed, pair)
    loads[5].wait()
    apply([rhs], [m0], [back_a])
    apply([m0], [n0], [back_b])
    weight_a = dot_sum(m0, rhs) / dot_sum(m0, m0)
    r1[...] = rhs[...] - weight_a * m0[...]
    m1[...] = m0[...] - weight_a * n0[...]
    weight_b = dot_sum(m1, r1) / dot_sum(m1, m1)
    near, deep = weight_a + weight_b, weight_a * weight_b
    d0[...] = weight_a * rhs[...] + weight_b * r1[...]
    pl.semaphore_wait(barrier, len(greeted))
    send_fields(0, d0)
    send_backs(0, lambda at: near * back_a[at] - deep * back_b[at])
    z_field[...] = weight_a * m0[...] + weight_b * m1[...]
    halo_finish(z_field, lambda d, kind: received(0, d, kind))

    part_zr, part_zz = dot_sum(z_field, rhs), dot_sum(z_field, z_field)
    gram = []

    def in_column_stage():
        apply([z_field], [lz], [back_c])
        apply([lz], [lz2], [back_d])
        centre = jnp.where(part_zz > 0.0, part_zr / jnp.where(part_zz > 0.0, part_zz, 1.0), 0.0)
        rt[...] = rhs[...] - centre * z_field[...]
        lt[...] = m0[...] - centre * lz[...]
        lt2[...] = n0[...] - centre * lz2[...]
        gram.extend([
            centre,
            dot_sum(lt, rt), dot_sum(lt, z_field) + dot_sum(lz, rt), dot_sum(lz, z_field),
            dot_sum(lt, lt), 2.0 * dot_sum(lt, lz), dot_sum(lz, lz),
            dot_sum(lt2, rt), dot_sum(lt2, z_field) + dot_sum(lz2, rt), dot_sum(lz2, z_field),
            dot_sum(lt2, lt), dot_sum(lt2, lz) + dot_sum(lz2, lt), dot_sum(lz2, lz),
            dot_sum(lt2, lt2), 2.0 * dot_sum(lt2, lz2), dot_sum(lz2, lz2),
        ])

    sums = mesh_sum(0, to_row([part_zr, part_zz]), (None, in_column_stage))
    sum_zz = from_row(sums, 1)
    alpha = from_row(sums, 0) / sum_zz
    near, deep = smoothing_weights(gram, alpha)
    r1[...] = rhs[...] - alpha * z_field[...]
    lt[...] = m0[...] - alpha * lz[...]
    d1[...] = near * r1[...] - deep * lt[...]
    send_fields(1, d1)
    send_backs(1, lambda at: near * (back_a[at] - alpha * back_c[at]) - deep * (back_b[at] - alpha * back_d[at]))
    raw[...] = near * lt[...] - deep * (n0[...] - alpha * lz2[...])
    halo_finish(raw, lambda d, kind: received(1, d, kind))

    columns = [dot_sum(z_field, raw), dot_sum(raw, r1), dot_sum(raw, raw), dot_sum(z_field, r1)]
    outs = [pltpu.make_async_copy(source, place_out, load_sem.at[k])
            for k, (source, place_out) in enumerate(((rt, pair_out), (lt2, zero_out), (r1, left_out)))]

    def in_last_stage():
        rt[...] = jnp.where(lower, d0[...], d1[...])
        lt2[...] = jnp.where(lower, z_field[...], raw[...])
        for out in outs:
            out.start()

    sums = mesh_sum(1, to_row(columns), (None, in_last_stage))
    cross, onto, square, kept = [from_row(sums, k) for k in range(4)]
    beta = cross / sum_zz
    alpha_b = (onto - beta * kept) / (square - beta * (2.0 * cross - beta * sum_zz))
    half = lane_r < 64
    scale_out[0] = jnp.where(half, alpha - alpha_b * beta, alpha_b)
    scale_out[1] = jnp.where(half, alpha_b * beta, -alpha_b)

    for out in outs:
        out.wait()
    for around in range(2):
        for d in range(4):
            for kind in range(2):
                halo_copy(around, d, kind).wait_send()
    for around in range(2):
        for index in range(len(STAGES)):
            for copy in sum_copies(around, index):
                copy.wait_send()


def combine(pair_ref, zero_ref, left_ref, scale_ref, sol_ref, res_ref):
    first = scale_ref[0] * pair_ref[...]
    second = scale_ref[1] * zero_ref[...]
    sol_ref[...] = (first + turned(first))[..., :64]
    res_ref[...] = (left_ref[...] + (second + turned(second)))[..., :64]


def solution(mesh):
    sizes = dict(mesh.shape)
    row_len = min(8, max(2, sizes["gx"] // 8))

    def step(rhs, self_coupling, hopping):
        field = EXT + (8, 64)
        vmem = pl.BlockSpec(memory_space=pltpu.VMEM)
        hbm = pl.BlockSpec(memory_space=pl.ANY)
        fields = [pltpu.VMEM(EXT + (8, 128), F32)] * 14
        backs = [pltpu.VMEM(EXT + (8, 256), F32)] * 5
        parts = pl.pallas_call(
            functools.partial(on_device, sizes, row_len),
            out_shape=[jax.ShapeDtypeStruct(EXT + (8, 128), F32)] * 3 + [jax.ShapeDtypeStruct((2, 8, 128), F32)],
            in_specs=[hbm] * 3,
            out_specs=[hbm] * 3 + [vmem],
            scratch_shapes=[
                pltpu.VMEM(field, F32),
                pltpu.VMEM(EXT + (64, 64), BF16),
                pltpu.VMEM((4,) + EXT + (64, 64), BF16),
                pltpu.VMEM(EXT + (64, 256), BF16),
                pltpu.VMEM(EXT + (16, 128), F32),
                pltpu.VMEM(EXT + (8, 64), F32),
                *backs,
                *fields,
                pltpu.VMEM((2, 2, 2, 16, 8, 128), BF16),
                pltpu.VMEM((2, 2, 2, 8, 8, 128), BF16),
                pltpu.VMEM((2, 2, 2, 16, 8, 128), BF16),
                pltpu.VMEM((2, 2, 2, 8, 8, 128), BF16),
                pltpu.VMEM((8, 1, 128), F32),
                pltpu.VMEM((2 * SLOTS, 1, 128), F32),
                pltpu.SemaphoreType.DMA((6,)),
                pltpu.SemaphoreType.DMA((16,)),
                pltpu.SemaphoreType.DMA((16,)),
                pltpu.SemaphoreType.DMA((2 * SLOTS,)),
                pltpu.SemaphoreType.DMA((2 * SLOTS,)),
            ],
            compiler_params=pltpu.CompilerParams(collective_id=0, has_side_effects=True),
        )(rhs[0], self_coupling[0], hopping[:, 0])
        sol, res = pl.pallas_call(
            combine,
            out_shape=[jax.ShapeDtypeStruct(field, F32)] * 2,
            in_specs=[vmem] * 4,
            out_specs=[vmem] * 2,
        )(*parts)
        return sol[None], res[None]

    whole_spec = P("gx", None, None, "gz", "ta", None, None)
    return jax.shard_map(
        step,
        mesh=mesh,
        in_specs=(whole_spec, whole_spec, P(None, "gx", None, None, "gz", "ta", None, None)),
        out_specs=(whole_spec, whole_spec),
        check_vma=False,
    )
```

```python
import functools

import jax
import jax.numpy as jnp
from jax import lax
from jax.experimental import pallas as pl
from jax.experimental.pallas import tpu as pltpu
from jax.sharding import PartitionSpec as P

MESH = pl.DeviceIdType.MESH
EXT = (2, 2, 4, 4)
F32 = jnp.float32
BF16 = jnp.bfloat16
STAGES = (1, 15, 31)
SLOTS = sum(STAGES)


def part(direction, low, high):
    return tuple(slice(low, high) if d == direction else slice(None) for d in range(4))


def flat(values):
    return values.reshape((-1,) + values.shape[4:])


def forward_dot(fields, links):
    return lax.dot_general(fields, links, (((2,), (2,)), ((0,), (0,))), preferred_element_type=F32)


def backward_dot(fields, links):
    return lax.dot_general(fields, links, (((2,), (1,)), ((0,), (0,))), preferred_element_type=F32)


def whole(mesh_size, value):
    return lax.rem(value + mesh_size, mesh_size)


class Place:
    def __init__(self, sizes, row_len):
        self.sizes = sizes
        self.row_len = row_len
        self.gx = lax.axis_index("gx")
        self.gz = lax.axis_index("gz")
        self.ta = lax.axis_index("ta")

    def at(self, gx=0, gz=0, ta=0, flip_gx=0, flip_ta=0):
        x = whole(self.sizes["gx"], self.gx + gx)
        z = whole(self.sizes["gz"], self.gz + gz)
        t = whole(self.sizes["ta"], self.ta + ta)
        if flip_gx:
            x = x + 1 - 2 * lax.rem(x, 2)
        if flip_ta & 1:
            t = t + 1 - 2 * lax.rem(t, 2)
        if flip_ta & 2:
            t = whole(self.sizes["ta"], t + 2)
        return {"gx": x, "gz": z, "ta": t}

    def ahead(self, direction, sign):
        if direction == 0:
            return self.at(gx=sign * self.row_len)
        if direction == 1:
            return self.at(gx=sign)
        if direction == 2:
            return self.at(gz=sign)
        return self.at(ta=sign)

    def stage(self, index):
        if index == 0:
            return [self.at(flip_ta=1)]
        if index == 1:
            turns = [(a, c, k) for k in (2, 1, 3, 0) for a in (1, 0) for c in (2, 0)]
            return [self.at(gz=k, flip_gx=a, flip_ta=c) for a, c, k in turns[:-1]]
        far = [16] + [sign * k for k in range(15, 0, -1) for sign in (1, -1)]
        return [self.at(gx=2 * k) for k in far]


def twice(values):
    return jnp.concatenate([values, values], axis=-1)


def turned(values):
    return pltpu.roll(values, 64, values.ndim - 1)


def groups():
    return [(x, y, z) for x in range(EXT[0]) for y in range(EXT[1]) for z in range(EXT[2])]


def signs():
    lane = lax.broadcasted_iota(jnp.int32, (1, 1, 128), 2)
    return jnp.where(lax.rem(lane, 64) < 32, 1.0, -1.0).astype(F32), lane < 64


def pack_links(hops, packed, pair):
    for g in groups():
        packed[g + (slice(None), slice(None), slice(128 * pair, 128 * pair + 128))] = jnp.concatenate(
            [hops[(2 * pair,) + g], hops[(2 * pair + 1,) + g]], axis=-1
        )


def local_apply(fields, outs, backs, links, packed, split, ahead_sum):
    chi, lower = signs()
    height = 16 * len(fields)
    rows = slice(0, height)
    for k, field in enumerate(fields):
        top = field[...].astype(BF16).astype(F32)
        split[..., 16 * k : 16 * k + 8, :] = top
        split[..., 16 * k + 8 : 16 * k + 16, :] = field[...] - top
    nil = jnp.zeros((4, height, 128), F32)
    for x, y, z in groups():
        own = split[x, y, z, :, rows, :]
        in_x = split[1, y, z, :, rows, :] if x == 0 else nil
        in_y = split[x, 1, z, :, rows, :] if y == 0 else nil
        in_z = split[x, y, z + 1, :, rows, :] if z < 3 else nil
        in_t = jnp.concatenate([own[1:], nil[:1]], axis=0)
        ahead = jnp.concatenate(
            [jnp.where(lower, in_x, in_y).astype(BF16), jnp.where(lower, in_z, in_t).astype(BF16)], axis=-1
        )
        onward = forward_dot(ahead, packed[x, y, z])
        onward = onward + forward_dot(own[..., :64].astype(BF16), links[x, y, z])
        back = backward_dot((own * chi)[..., :64].astype(BF16), packed[x, y, z])
        for k in range(len(fields)):
            a, b = slice(16 * k, 16 * k + 8), slice(16 * k + 8, 16 * k + 16)
            ahead_sum[x, y, z, :, 8 * k : 8 * k + 8, :] = onward[:, a] + onward[:, b]
            backs[k][x, y, z] = back[:, a] + back[:, b]
    nil = jnp.zeros((4, 8, 128), F32)
    for k, (field, out) in enumerate(zip(fields, outs)):
        for x, y, z in groups():
            first, second = slice(0, 128), slice(128, 256)
            in_x = backs[k][0, y, z, :, :, first] if x else nil
            in_y = backs[k][x, 0, z, :, :, first] if y else nil
            in_z = backs[k][x, y, z - 1, :, :, second] if z else nil
            in_t = jnp.concatenate([nil[:1], backs[k][x, y, z, 0:3, :, second]], axis=0)
            total = chi * (jnp.where(lower, in_x, in_y) + jnp.where(lower, in_z, in_t))
            onward = ahead_sum[x, y, z, :, 8 * k : 8 * k + 8, :]
            total = total + jnp.concatenate([onward, jnp.zeros_like(onward)], axis=-1)
            out[x, y, z] = 4.0 * field[x, y, z] + (total + turned(total))


def on_device(sizes, row_len, rhs_hbm, self_hbm, hop_hbm, pair_out, zero_out, left_out, scale_out,
              rhs_in, links, hops, packed, split, ahead_sum, back_a, back_b, back_c, back_d, halo_in,
              rhs, m0, m1, r1, d0, z_field, rt, lt, lz, lt2, lz2, d1,
              send_xy, send_zt, got_xy, got_zt, rows_out, rows_in,
              load_sem, halo_send, halo_recv, sum_send, sum_recv):
    place = Place(sizes, row_len)
    loads = [pltpu.make_async_copy(rhs_hbm, rhs_in, load_sem.at[0])]
    for d in range(4):
        loads.append(pltpu.make_async_copy(hop_hbm.at[d], hops.at[d], load_sem.at[1 + d]))
    loads.append(pltpu.make_async_copy(self_hbm, links, load_sem.at[5]))
    for load in loads:
        load.start()

    greeted = [place.ahead(d, sign) for d in range(4) for sign in (1, -1)]
    for index in range(len(STAGES)):
        greeted += place.stage(index)
    barrier = pltpu.get_barrier_semaphore()
    for other in greeted:
        pl.semaphore_signal(barrier, inc=1, device_id=other, device_id_type=MESH)

    chi, lower = signs()
    lane_r = lax.broadcasted_iota(jnp.int32, (8, 128), 1)
    sub_r = lax.broadcasted_iota(jnp.int32, (8, 128), 0)

    def dot_sum(a, b):
        summed = jnp.sum(flat(a[...]) * flat(b[...]), axis=0)
        return jnp.sum(summed[:, :64], axis=-1, keepdims=True)

    def to_row(columns):
        spread = jnp.zeros((8, 128), F32)
        for k, column in enumerate(columns):
            spread = jnp.where(lane_r == 8 * k + sub_r, column, spread)
        return jnp.sum(spread, axis=0, keepdims=True)

    def from_row(row, k):
        return jnp.sum(jnp.where(lane_r == 8 * k + sub_r, row, 0.0), axis=1, keepdims=True)

    def apply(fields, outs, backs):
        local_apply(fields, outs, backs, links, packed, split, ahead_sum)

    def face_ref(store, around, d, kind):
        xy, zt = store
        return (xy if d < 2 else zt).at[around, d % 2, kind]

    def halo_copy(around, d, kind):
        slot = (around * 4 + d) * 2 + kind
        return pltpu.make_async_remote_copy(
            src_ref=face_ref((send_xy, send_zt), around, d, kind),
            dst_ref=face_ref((got_xy, got_zt), around, d, kind),
            send_sem=halo_send.at[slot],
            recv_sem=halo_recv.at[slot],
            device_id=place.ahead(d, -1 if kind == 0 else 1),
            device_id_type=MESH,
        )

    def halo_start(around, field, back_of):
        for d in range(4):
            low = flat(field[part(d, 0, 1)])
            half = low.shape[0] // 2
            face_ref((send_xy, send_zt), around, d, 0)[...] = jnp.where(lower, low[:half], low[half:]).astype(BF16)
            halo_copy(around, d, 0).start()
            lanes = slice(128 * (d // 2), 128 * (d // 2) + 128)
            back = flat(chi * back_of(part(d, EXT[d] - 1, EXT[d]) + (slice(None), lanes)))
            if d % 2:
                back = jnp.where(lower, turned(back[:half]), back[half:])
            else:
                back = jnp.where(lower, back[:half], turned(back[half:]))
            face_ref((send_xy, send_zt), around, d, 1)[...] = back.astype(BF16)
            halo_copy(around, d, 1).start()

    def halo_finish(around, out):
        for d in (2, 3, 1, 0):
            shape = tuple(1 if k == d else EXT[k] for k in range(4)) + (8, 128)
            halo_copy(around, d, 0).wait_recv()
            got = face_ref((got_xy, got_zt), around, d, 0)[...].astype(F32)
            pieces = (turned(got), got) if d % 2 else (got, turned(got))
            lanes = slice(64 * (d % 2), 64 * (d % 2) + 64)
            place_in = slice(64 * d, 64 * d + 64)
            field = jnp.concatenate(pieces, axis=0).reshape(shape)[..., lanes]
            halo_in[part(d, EXT[d] - 1, EXT[d]) + (slice(None), place_in)] = field
            halo_copy(around, d, 1).wait_recv()
            got = face_ref((got_xy, got_zt), around, d, 1)[...].astype(F32)
            other = turned(got)
            both = jnp.concatenate([jnp.where(lower, got, other), jnp.where(lower, other, got)], axis=0)
            out[part(d, 0, 1)] += both.reshape(shape)
        for g in groups():
            onward = forward_dot(halo_in[g].astype(BF16), packed[g])
            out[g] += twice(onward)

    def sum_copies(around, index):
        base = around * SLOTS + sum(STAGES[:index])
        return [
            pltpu.make_async_remote_copy(
                src_ref=rows_out.at[around * 4 + index],
                dst_ref=rows_in.at[base + k],
                send_sem=sum_send.at[base + k],
                recv_sem=sum_recv.at[base + k],
                device_id=other,
                device_id_type=MESH,
            )
            for k, other in enumerate(place.stage(index))
        ]

    def mesh_sum(around, row, meanwhile=None):
        for index in range(len(STAGES)):
            base = around * SLOTS + sum(STAGES[:index])
            rows_out[around * 4 + index] = row
            copies = sum_copies(around, index)
            for copy in copies:
                copy.start()
            if index == len(STAGES) - 1 and meanwhile is not None:
                meanwhile()
            for copy in copies:
                copy.wait_recv()
            row = row + jnp.sum(rows_in[base : base + len(copies)], axis=0)
        return row

    halo_in[...] = jnp.zeros_like(halo_in)
    loads[0].wait()
    rhs[...] = twice(rhs_in[...])
    for pair in range(2):
        loads[1 + 2 * pair].wait()
        loads[2 + 2 * pair].wait()
        pack_links(hops, packed, pair)
    loads[5].wait()
    apply([rhs], [m0], [back_a])
    weight_a = dot_sum(m0, rhs) / dot_sum(m0, m0)
    r1[...] = rhs[...] - weight_a * m0[...]
    apply([r1], [m1], [back_b])
    weight_b = dot_sum(m1, r1) / dot_sum(m1, m1)
    d0[...] = weight_a * rhs[...] + weight_b * r1[...]
    pl.semaphore_wait(barrier, len(greeted))
    halo_start(0, d0, lambda at: weight_a * back_a[at] + weight_b * back_b[at])
    z_field[...] = weight_a * m0[...] + weight_b * m1[...]
    halo_finish(0, z_field)

    part_zr, part_zz = dot_sum(z_field, rhs), dot_sum(z_field, z_field)
    centre = jnp.where(part_zz > 0.0, part_zr / jnp.where(part_zz > 0.0, part_zz, 1.0), 0.0)

    def meanwhile():
        rt[...] = rhs[...] - centre * z_field[...]
        apply([rt, z_field], [lt, lz], [back_a, back_b])
        apply([lt, lz], [lt2, lz2], [back_c, back_d])

    sums = mesh_sum(0, to_row([part_zr, part_zz]), meanwhile)
    sum_zz = from_row(sums, 1)
    alpha = from_row(sums, 0) / sum_zz
    shift = alpha - centre
    r1[...] = rhs[...] - alpha * z_field[...]
    m0[...] = lt[...] - shift * lz[...]
    weight_a = dot_sum(m0, r1) / dot_sum(m0, m0)
    m1[...] = m0[...] - weight_a * (lt2[...] - shift * lz2[...])
    rt[...] = r1[...] - weight_a * m0[...]
    weight_b = dot_sum(m1, rt) / dot_sum(m1, m1)
    d1[...] = weight_a * r1[...] + weight_b * rt[...]
    near = weight_a + weight_b
    deep = weight_a * weight_b

    def back_of(at):
        return near * (back_a[at] - shift * back_b[at]) - deep * (back_c[at] - shift * back_d[at])

    halo_start(1, d1, back_of)
    lz[...] = weight_a * m0[...] + weight_b * m1[...]
    halo_finish(1, lz)

    columns = [dot_sum(z_field, lz), dot_sum(lz, r1), dot_sum(lz, lz), dot_sum(z_field, r1)]
    outs = [pltpu.make_async_copy(source, place_out, load_sem.at[k])
            for k, (source, place_out) in enumerate(((rt, pair_out), (lt2, zero_out), (r1, left_out)))]

    def in_last_stage():
        rt[...] = jnp.where(lower, d0[...], d1[...])
        lt2[...] = jnp.where(lower, z_field[...], lz[...])
        for out in outs:
            out.start()

    sums = mesh_sum(1, to_row(columns), in_last_stage)
    cross, onto, square, kept = [from_row(sums, k) for k in range(4)]
    beta = cross / sum_zz
    alpha_b = (onto - beta * kept) / (square - beta * (2.0 * cross - beta * sum_zz))
    half = lane_r < 64
    scale_out[0] = jnp.where(half, alpha - alpha_b * beta, alpha_b)
    scale_out[1] = jnp.where(half, alpha_b * beta, -alpha_b)

    for out in outs:
        out.wait()
    for around in range(2):
        for d in range(4):
            for kind in range(2):
                halo_copy(around, d, kind).wait_send()
        for index in range(len(STAGES)):
            for copy in sum_copies(around, index):
                copy.wait_send()


def combine(pair_ref, zero_ref, left_ref, scale_ref, sol_ref, res_ref):
    first = scale_ref[0] * pair_ref[...]
    second = scale_ref[1] * zero_ref[...]
    sol_ref[...] = (first + turned(first))[..., :64]
    res_ref[...] = (left_ref[...] + (second + turned(second)))[..., :64]


def solution(mesh):
    sizes = dict(mesh.shape)
    row_len = min(8, max(2, sizes["gx"] // 8))

    def step(rhs, self_coupling, hopping):
        field = EXT + (8, 64)
        vmem = pl.BlockSpec(memory_space=pltpu.VMEM)
        hbm = pl.BlockSpec(memory_space=pl.ANY)
        fields = [pltpu.VMEM(EXT + (8, 128), F32)] * 12
        backs = [pltpu.VMEM(EXT + (8, 256), F32)] * 5
        parts = pl.pallas_call(
            functools.partial(on_device, sizes, row_len),
            out_shape=[jax.ShapeDtypeStruct(EXT + (8, 128), F32)] * 3 + [jax.ShapeDtypeStruct((2, 8, 128), F32)],
            in_specs=[hbm] * 3,
            out_specs=[hbm] * 3 + [vmem],
            scratch_shapes=[
                pltpu.VMEM(field, F32),
                pltpu.VMEM(EXT + (64, 64), BF16),
                pltpu.VMEM((4,) + EXT + (64, 64), BF16),
                pltpu.VMEM(EXT + (64, 256), BF16),
                pltpu.VMEM(EXT + (32, 128), F32),
                pltpu.VMEM(EXT + (16, 64), F32),
                *backs,
                *fields,
                pltpu.VMEM((2, 2, 2, 16, 8, 128), BF16),
                pltpu.VMEM((2, 2, 2, 8, 8, 128), BF16),
                pltpu.VMEM((2, 2, 2, 16, 8, 128), BF16),
                pltpu.VMEM((2, 2, 2, 8, 8, 128), BF16),
                pltpu.VMEM((8, 1, 128), F32),
                pltpu.VMEM((2 * SLOTS, 1, 128), F32),
                pltpu.SemaphoreType.DMA((6,)),
                pltpu.SemaphoreType.DMA((16,)),
                pltpu.SemaphoreType.DMA((16,)),
                pltpu.SemaphoreType.DMA((2 * SLOTS,)),
                pltpu.SemaphoreType.DMA((2 * SLOTS,)),
            ],
            compiler_params=pltpu.CompilerParams(collective_id=0, has_side_effects=True),
        )(rhs[0], self_coupling[0], hopping[:, 0])
        sol, res = pl.pallas_call(
            combine,
            out_shape=[jax.ShapeDtypeStruct(field, F32)] * 2,
            in_specs=[vmem] * 4,
            out_specs=[vmem] * 2,
        )(*parts)
        return sol[None], res[None]

    whole_spec = P("gx", None, None, "gz", "ta", None, None)
    return jax.shard_map(
        step,
        mesh=mesh,
        in_specs=(whole_spec, whole_spec, P(None, "gx", None, None, "gz", "ta", None, None)),
        out_specs=(whole_spec, whole_spec),
        check_vma=False,
    )
```
